32 devices in a mesh: dp: 4 (over y, x), seq: 4 (over z), fsdp: 2 (over core).
Axes of the slice: x: 2, y: 2, z: 4, core: 2. Of those that a mesh axis runs over, the one named last changes fastest.
Arguments:
- inputs: bfloat16 [8, 1536, 1024], P(('dp', 'fsdp'), 'seq'), may hold values from -6 to 6
- doc_ids: int32 [8, 1536], P(('dp', 'fsdp'), 'seq'), may hold values from 0 to 1, never falling along the last dimension, each value on 1 to 1535 neighbouring positions
- timesteps: int32 [8], P(('dp', 'fsdp')), may hold values from 0 to 4999
- query_weight: bfloat16 [1024, 1024], P('fsdp'), may hold values from -0.1875 to 0.1875
- query_bias: bfloat16 [1024], P('fsdp'), may hold values from -1.75 to 1.75
- key_weight: bfloat16 [1024, 1024], P('fsdp'), may hold values from -0.1875 to 0.1875
- value_weight: bfloat16 [1024, 1024], P('fsdp'), may hold values from -0.1875 to 0.1875
- value_bias: bfloat16 [1024], P('fsdp'), may hold values from -1.75 to 1.75
- out_weight: bfloat16 [1024, 1024], P('fsdp'), may hold values from -2 to 2
- out_bias: bfloat16 [1024], P('fsdp'), may hold values from -1.75 to 1.75
- first_gain: bfloat16 [1024], P('fsdp'), may hold values from 0.5 to 1.5
- first_shift: bfloat16 [1024], P('fsdp'), may hold values from -1.75 to 1.75
- inner_weight: bfloat16 [1024, 4096], P('fsdp'), may hold values from -0.1875 to 0.1875
- inner_bias: bfloat16 [4096], P('fsdp'), may hold values from -1.75 to 1.75
- outer_weight: bfloat16 [4096, 1024], P('fsdp'), may hold values from -0.09375 to 0.09375
- outer_bias: bfloat16 [1024], P('fsdp'), may hold values from -1.75 to 1.75
- second_gain: bfloat16 [1024], P('fsdp'), may hold values from 0.5 to 1.5
- second_shift: bfloat16 [1024], P('fsdp'), may hold values from -1.75 to 1.75
- time_weight: bfloat16 [1024, 1024], P('fsdp'), may hold values from -0.1875 to 0.1875
- time_bias: bfloat16 [1024], P('fsdp'), may hold values from -1.75 to 1.75
- cotangent: bfloat16 [8, 1536, 1024], P(('dp', 'fsdp'), 'seq'), may hold values from -6 to 6
Outputs:
- output: bfloat16 [8, 1536, 1024], P(('dp', 'fsdp'), 'seq')
- input_grad: bfloat16 [8, 1536, 1024], P(('dp', 'fsdp'), 'seq')
- query_weight_grad: float32 [1024, 1024], P('fsdp')
- query_bias_grad: float32 [1024], P('fsdp')
- key_weight_grad: float32 [1024, 1024], P('fsdp')
- value_weight_grad: float32 [1024, 1024], P('fsdp')
- value_bias_grad: float32 [1024], P('fsdp')
- out_weight_grad: float32 [1024, 1024], P('fsdp')
- out_bias_grad: float32 [1024], P('fsdp')
- first_gain_grad: float32 [1024], P('fsdp')
- first_shift_grad: float32 [1024], P('fsdp')
- inner_weight_grad: float32 [1024, 4096], P('fsdp')
- inner_bias_grad: float32 [4096], P('fsdp')
- outer_weight_grad: float32 [4096, 1024], P('fsdp')
- outer_bias_grad: float32 [1024], P('fsdp')
- second_gain_grad: float32 [1024], P('fsdp')
- second_shift_grad: float32 [1024], P('fsdp')
- time_weight_grad: float32 [1024, 1024], P('fsdp')
- time_bias_grad: float32 [1024], P('fsdp')
The draws below stay inside these ranges and needn't reach their ends.
Inputs may be any that keep to these rules, and one draw needn't show every extreme that they name: `doc_ids`: within a sequence the document numbers never fall; there are 2 documents of 1 to 1535 tokens each.
All inputs are finite; a program needn't handle non-finite values.
Results may differ from the reference program's by a relative error of at most 0.019.
The reference program's roundings to bfloat16 on the way count: a program that leaves them out, or rounds other values in their place, can miss the bound.
Values may be sent and summed in bfloat16 or wider, within the bound.
No kernel may reach another device: no remote copies, remote signals or barrier semaphores. Data moves between devices by JAX's collectives and lax.ppermute only.
A program may use at most 192 MiB of HBM per device.

```python
import math
import jax
import jax.numpy as jnp
import numpy as np
from jax import lax

D = 1024
H = 16
FF = 4096
DH = 64
LEN = 1536
SEQS = 8
DOCS = 2
MOST = 1535


def with_ends(array, key, smallest, top_value):
    longest = array.shape.index(max(array.shape))
    spots = []
    for shift in (0, 1):
        where = [jax.random.randint(jax.random.fold_in(key, axis), (), 0, length) for axis, length in enumerate(array.shape)]
        where[longest] = (where[longest] + shift) % array.shape[longest]
        spots.append(tuple(where))
    return array.at[spots[0]].set(smallest).at[spots[1]].set(top_value)


def with_spikes(array, stream_key, source, target, blocks, factor):
    def block_of(axis_at):
        return (jnp.arange(array.shape[axis_at]) // (array.shape[axis_at] // blocks)).reshape((-1,) + (1,) * (array.ndim - 1 - axis_at))

    near = jax.random.permutation(stream_key, blocks)[block_of(target)]
    far = (block_of(target) + blocks // 2) % blocks
    return jnp.where((block_of(source) == near) | (block_of(source) == far), factor * array, array)


def shard_levels(rng, dims, split, least, top_value):
    factor_of, own = 1.0, jax.random.fold_in(rng, 6)
    for position, shards_of in split:
        heights = jnp.exp(jax.random.uniform(jax.random.fold_in(own, position), (shards_of,), jnp.float32, least / len(split), top_value / len(split)))
        factor_of = factor_of * jnp.repeat(heights, dims[position] // shards_of).reshape([-1 if axis == position else 1 for axis in range(len(dims))])
    return factor_of


def split_up(count, total, limit, skew):
    portions = [(1 << 20) // math.isqrt(rank ** skew) + 1 for rank in range(2, count + 1)]
    spare, holding = total - limit - (count - 1), [1] * (count - 1)
    while spare > 0:
        movable = [i for i in range(count - 1) if holding[i] < limit]
        mass, remaining = sum([portions[i] for i in movable]), spare
        for i in movable:
            extra = min(limit - holding[i], max(1, remaining * portions[i] // mass), spare)
            holding[i] = holding[i] + extra
            spare = spare - extra
    return np.array([limit] + holding)


def ragged(stream_key, number_of, total, limit, slope):
    if number_of == 2:
        one = jax.random.randint(stream_key, (), max(1, total - limit), min(limit, total - 1) + 1)
        return jnp.stack([one, total - one])
    lengths = jnp.asarray(split_up(number_of, total, limit, slope), jnp.int32)
    twos = (number_of - 1) // 2
    donor, taker = lengths[1:1 + 2 * twos:2], lengths[2:2 + 2 * twos:2]
    room = jnp.minimum(donor - 1, limit - taker)
    shifted = jax.random.randint(jax.random.fold_in(stream_key, 1), (twos,), 0, 1 << 20) % (room + 1)
    lengths = lengths.at[1:1 + 2 * twos:2].set(donor - shifted).at[2:2 + 2 * twos:2].set(taker + shifted)
    return lengths[jax.random.permutation(jax.random.fold_in(stream_key, 2), number_of)]


def centred(stream_key, extent, scale, most, cuts=(), kind=jnp.bfloat16):
    array = jax.random.normal(stream_key, extent, jnp.float32) * scale
    if len(cuts) > 0:
        array = shard_levels(stream_key, extent, cuts, -0.22, 0.18) * array
    return jnp.clip(array, min=-most, max=most).astype(kind)


def bell_draw_with(own_key, extent, width, reach, split, heavy, kind=jnp.bfloat16):
    array = width * jax.random.normal(own_key, extent, jnp.float32)
    if split:
        array = array * shard_levels(own_key, extent, split, -0.22, 0.18)
    return jnp.clip(with_spikes(array, jax.random.fold_in(own_key, 3), *heavy), -reach, reach).astype(kind)


def setup_inputs(seed: int = 0) -> dict:
    seeds = jax.random.split(jax.random.key(seed), 22)
    inputs = bell_draw_with(seeds[0], (SEQS, LEN, D), 1.0, 6.0, ((0, 8), (1, 4)), (1, 2, 4, 2.0))
    doc_ids = jax.vmap(lambda own: jnp.searchsorted(jnp.cumsum(ragged(own, DOCS, LEN, MOST, 1)), jnp.arange(LEN), side="right"))(jax.random.split(seeds[1], SEQS)).reshape((SEQS, LEN)).astype(jnp.int32)
    timesteps = with_ends(jax.random.randint(seeds[2], (SEQS,), 0, 5000), jax.random.fold_in(seeds[2], 1), 0, 4999).astype(jnp.int32)
    query_weight = centred(seeds[3], (D, D), D ** -0.5, 0.1875, ((0, 2),))
    query_bias = centred(seeds[4], (D,), 0.3, 1.75, ((0, 2),))
    key_weight = centred(seeds[5], (D, D), D ** -0.5, 0.1875, ((0, 2),))
    value_weight = centred(seeds[6], (D, D), D ** -0.5, 0.1875, ((0, 2),))
    value_bias = centred(seeds[7], (D,), 0.3, 1.75, ((0, 2),))
    out_weight = centred(seeds[8], (D, D), (max(1, D // 128)) ** -0.5, 2.0, ((0, 2),))
    out_bias = centred(seeds[9], (D,), 0.3, 1.75, ((0, 2),))
    first_gain = jnp.clip(1.0 + 0.1 * jax.random.normal(seeds[10], (D,), jnp.float32), 0.5, 1.5).astype(jnp.bfloat16)
    first_shift = centred(seeds[11], (D,), 0.3, 1.75, ((0, 2),))
    inner_weight = centred(seeds[12], (D, FF), D ** -0.5, 0.1875, ((0, 2),))
    inner_bias = centred(seeds[13], (FF,), 0.3, 1.75, ((0, 2),))
    outer_weight = centred(seeds[14], (FF, D), FF ** -0.5, 0.09375, ((0, 2),))
    outer_bias = centred(seeds[15], (D,), 0.3, 1.75, ((0, 2),))
    second_gain = jnp.clip(1.0 + 0.1 * jax.random.normal(seeds[16], (D,), jnp.float32), 0.5, 1.5).astype(jnp.bfloat16)
    second_shift = centred(seeds[17], (D,), 0.3, 1.75, ((0, 2),))
    time_weight = centred(seeds[18], (D, D), D ** -0.5, 0.1875, ((0, 2),))
    time_bias = centred(seeds[19], (D,), 0.3, 1.75, ((0, 2),))
    cotangent = centred(seeds[20], (SEQS, LEN, D), 1.0, 6.0, ((0, 8), (1, 4)))
    return {"inputs": inputs, "doc_ids": doc_ids, "timesteps": timesteps, "query_weight": query_weight, "query_bias": query_bias, "key_weight": key_weight, "value_weight": value_weight, "value_bias": value_bias, "out_weight": out_weight, "out_bias": out_bias, "first_gain": first_gain, "first_shift": first_shift, "inner_weight": inner_weight, "inner_bias": inner_bias, "outer_weight": outer_weight, "outer_bias": outer_bias, "second_gain": second_gain, "second_shift": second_shift, "time_weight": time_weight, "time_bias": time_bias, "cotangent": cotangent}


epsilon = 1e-05
highest = lax.Precision.HIGHEST

@jax.custom_vjp
def low(v):
    return lax.optimization_barrier(v.astype(jnp.bfloat16)).astype(jnp.float32)

@jax.custom_vjp
def low_back(v):
    return v

def low_keep(v):
    return (low(v), None)

def low_pass(kept, grad):
    return (grad,)

def back_keep(v):
    return (v, None)

def back_low(kept, grad):
    return (low(grad),)
low.defvjp(low_keep, low_pass)
low_back.defvjp(back_keep, back_low)

def product(left, right):
    return jnp.dot(left, right, precision=highest)

def time_features(steps_given):
    half = D // 2
    frequency = np.exp(-math.log(10000.0) * np.arange(half) / half).astype(np.float32)
    angles = steps_given.astype(jnp.float32)[:, None] * jnp.asarray(frequency)[None, :]
    return jnp.concatenate([jnp.sin(angles), jnp.cos(angles)], axis=1)

def normalize(values, gain, shift):
    center = values - lax.optimization_barrier(jnp.mean(values, axis=-1, keepdims=True))
    spread = lax.optimization_barrier(jnp.mean(center * center, axis=-1, keepdims=True))
    return center * lax.rsqrt(spread + epsilon) * gain + shift

def attend(query, keys, values, segments):
    length = query.shape[0]
    block = min(512, length)
    count = length // block
    scale = 1.0 / math.sqrt(DH)
    key_heads = keys.reshape(length, H, DH)
    value_heads = values.reshape(length, H, DH)

    def one_block(item):
        query_block, segment_block = item
        scores = jnp.einsum('qhd,khd->hqk', query_block.reshape(block, H, DH), key_heads, precision=highest) * scale
        scores = low_back(scores)
        same_doc = (segment_block[:, None] == segments[None, :])[None]
        scores = jnp.where(same_doc, scores, -1000000000.0)
        highest_score = lax.optimization_barrier(jnp.max(scores, axis=-1, keepdims=True))
        expon = jnp.exp(scores - highest_score)
        shares = expon / lax.optimization_barrier(jnp.sum(expon, axis=-1, keepdims=True))
        mixed = jnp.einsum('hqk,khd->qhd', low(shares), value_heads, precision=highest)
        return mixed.reshape(block, H * DH)
    mixed = lax.map(jax.checkpoint(one_block), (query.reshape(count, block, H * DH), segments.reshape(count, block)))
    return mixed.reshape(length, H * DH)

def sequence_layer(parameters, item):
    query_matrix, query_offset, key_matrix, value_matrix, value_offset, out_matrix, out_offset, first_scale, first_offset, inner_matrix, inner_offset, outer_matrix, outer_offset, second_scale, second_offset, time_matrix, time_offset = parameters
    state, embedded, segments = item
    start = state + embedded[None, :]
    start_low = low(start)
    query = low(low_back(product(start_low, query_matrix) + query_offset))
    keys = low(low_back(product(start_low, key_matrix)))
    values = low(low_back(product(start_low, value_matrix) + value_offset))
    mixed = low(low_back(attend(query, keys, values, segments)))
    attended = low_back(product(mixed, out_matrix) + out_offset)
    first_out = normalize(start + attended, first_scale, first_offset)
    inner = low_back(product(low(first_out), inner_matrix) + inner_offset)
    activated = low(jax.nn.gelu(inner, approximate=False))
    outer = low_back(product(activated, outer_matrix) + outer_offset)
    return normalize(first_out + outer, second_scale, second_offset)

def layer(state, parameters, timesteps, doc_ids):
    features = low(time_features(timesteps))
    embedded = product(features, parameters[15]) + parameters[16]

    def per_sequence(item):
        return sequence_layer(parameters, item)
    return lax.map(per_sequence, (state, embedded, doc_ids))

def reference(inputs, doc_ids, timesteps, query_weight, query_bias, key_weight, value_weight, value_bias, out_weight, out_bias, first_gain, first_shift, inner_weight, inner_bias, outer_weight, outer_bias, second_gain, second_shift, time_weight, time_bias, cotangent):
    parameters = tuple((each.astype(jnp.float32) for each in (query_weight, query_bias, key_weight, value_weight, value_bias, out_weight, out_bias, first_gain, first_shift, inner_weight, inner_bias, outer_weight, outer_bias, second_gain, second_shift, time_weight, time_bias)))
    state = inputs.astype(jnp.float32)

    def forward(state_in, parameters_in):
        return layer(state_in, parameters_in, timesteps, doc_ids)
    output, backward = jax.vjp(forward, state, parameters)
    state_grad, grads = backward(cotangent.astype(jnp.float32))
    return (output.astype(jnp.bfloat16), state_grad.astype(jnp.bfloat16), grads[0], grads[1], grads[2], grads[3], grads[4], grads[5], grads[6], grads[7], grads[8], grads[9], grads[10], grads[11], grads[12], grads[13], grads[14], grads[15], grads[16])
```

```python
import math

import jax
import jax.numpy as jnp
import numpy as np
from jax import lax
from jax.experimental import pallas as pl
from jax.experimental.pallas import tpu as pltpu
from jax.sharding import PartitionSpec as P

D = 1024
DH = 64
LANES = 128
FAR = -1e30


epsilon = 1e-05


def time_features(steps_given):
    half = D // 2
    frequency = np.exp(-math.log(10000.0) * np.arange(half) / half).astype(np.float32)
    angles = steps_given.astype(jnp.float32)[:, None] * jnp.asarray(frequency)[None, :]
    return jnp.concatenate([jnp.sin(angles), jnp.cos(angles)], axis=1)


def normalize(values, gain, shift):
    center = values - jnp.mean(values, axis=-1, keepdims=True)
    spread = jnp.mean(center * center, axis=-1, keepdims=True)
    return center * lax.rsqrt(spread + epsilon) * gain + shift


def exact_gelu(values):
    return jax.nn.gelu(values, approximate=False)


def matmul(left, right):
    return lax.dot_general(
        left, right, (((1,), (0,)), ((), ())), preferred_element_type=jnp.float32
    )


def matmul_left(left, right):
    return lax.dot_general(
        left, right, (((0,), (0,)), ((), ())), preferred_element_type=jnp.float32
    )


def matmul_right(left, right):
    return lax.dot_general(
        left, right, (((1,), (1,)), ((), ())), preferred_element_type=jnp.float32
    )


def sides(segments):
    length = segments.shape[0]
    lane = lax.broadcasted_iota(jnp.int32, (length, LANES), 1)
    same = segments[:, None] == lane
    key_side = jnp.where(
        lane < 8, jnp.where(same, 0.0, FAR), jnp.where(lane < 11, 1.0, 0.0)
    ).astype(jnp.bfloat16)
    query_side = jnp.where((lane < 8) & same, 1.0, 0.0).astype(jnp.bfloat16)
    return key_side, query_side


def placed_offset(column, lane, base):
    high = column.astype(jnp.bfloat16).astype(jnp.float32)
    rest = column - high
    middle = rest.astype(jnp.bfloat16).astype(jnp.float32)
    low = rest - middle
    return jnp.where(
        lane == 8, -high, jnp.where(lane == 9, -middle, jnp.where(lane == 10, -low, base))
    )


def forward_kernel(length, rows):
    def kernel(query, keys, values, key_side, query_side, mixed, kept):
        lane = lax.broadcasted_iota(jnp.int32, (rows, LANES), 1)
        wide_keys = jnp.concatenate([keys[...], key_side[...]], axis=1)
        all_values = values[...]
        for step in range(length // rows):
            part = pl.ds(step * rows, rows)
            pair = query[part, :] * jnp.bfloat16(0.125)
            side = query_side[part, :]
            outs = []
            for head in range(2):
                mine = (lane < DH) if head == 0 else (lane >= DH)
                wide = jnp.concatenate([jnp.where(mine, pair, jnp.bfloat16(0)), side], axis=1)
                scores = matmul_right(wide, wide_keys)
                top = jnp.max(scores, axis=1, keepdims=True)
                expon = jnp.exp(scores - top)
                total = jnp.sum(expon, axis=1, keepdims=True)
                shares = (expon * (1.0 / total)).astype(jnp.bfloat16)
                outs.append(matmul(shares, all_values))
                kept[head, part, :] = placed_offset(
                    top + jnp.log(total), lane, side.astype(jnp.float32)
                ).astype(jnp.bfloat16)
            mixed[part, :] = jnp.where(lane < DH, outs[0], outs[1]).astype(jnp.bfloat16)

    return kernel


def fitting_rows(length):
    for rows in (512, 384, 256, 128):
        if length % rows == 0:
            return rows
    return length


def attend_forward(packed, pair, key_side, query_side):
    length = packed.shape[0]
    whole = pl.BlockSpec((length, LANES), lambda g: (0, 0))
    return pl.pallas_call(
        forward_kernel(length, fitting_rows(length)),
        grid=(1,),
        in_specs=[pl.BlockSpec((length, LANES), lambda g, i=i: (0, 3 * pair + i)) for i in range(3)]
        + [whole, whole],
        out_specs=[whole, pl.BlockSpec((2, length, LANES), lambda g: (0, 0, 0))],
        out_shape=[
            jax.ShapeDtypeStruct((length, LANES), jnp.bfloat16),
            jax.ShapeDtypeStruct((2, length, LANES), jnp.bfloat16),
        ],
        cost_estimate=pl.CostEstimate(
            flops=2 * 2 * length * length * 384,
            transcendentals=2 * length * length,
            bytes_accessed=length * LANES * 2 * 8,
        ),
        name="attend_forward",
    )(packed, packed, packed, key_side, query_side)


def backward_kernel(length, rows):
    def kernel(
        query, keys, values, key_side, kept, mixed, grad_mixed, grads, key_sum, value_sum
    ):
        lane = lax.broadcasted_iota(jnp.int32, (rows, LANES), 1)
        wide_keys = jnp.concatenate([keys[...], key_side[...]], axis=1)
        wide_values = jnp.concatenate([values[...], key_side[...]], axis=1)
        all_keys = keys[...]
        for step in range(length // rows):
            part = pl.ds(step * rows, rows)
            pair = query[part, :] * jnp.bfloat16(0.125)
            grad = grad_mixed[part, :]
            product = grad.astype(jnp.float32) * mixed[part, :].astype(jnp.float32)
            outs = []
            for head in range(2):
                mine = (lane < DH) if head == 0 else (lane >= DH)
                own_query = jnp.where(mine, pair, jnp.bfloat16(0))
                own_grad = jnp.where(mine, grad, jnp.bfloat16(0))
                centered = jnp.sum(jnp.where(mine, product, 0.0), axis=1, keepdims=True)
                side = placed_offset(centered, lane, 0.0).astype(jnp.bfloat16)
                scores = matmul_right(
                    wide_keys, jnp.concatenate([own_query, kept[head, part, :]], axis=1)
                )
                shares = jnp.exp(scores)
                share_grad = matmul_right(
                    wide_values, jnp.concatenate([own_grad, side], axis=1)
                )
                score_grad = (shares * share_grad).astype(jnp.bfloat16)
                low_shares = shares.astype(jnp.bfloat16)
                key_part = matmul(score_grad, own_query)
                value_part = matmul(low_shares, own_grad)
                if step == 0 and head == 0:
                    key_sum[...] = key_part
                    value_sum[...] = value_part
                else:
                    key_sum[...] += key_part
                    value_sum[...] += value_part
                outs.append(matmul_left(score_grad, all_keys))
            grads[part, :LANES] = (jnp.where(lane < DH, outs[0], outs[1]) * 0.125).astype(
                jnp.bfloat16
            )
        grads[:, LANES : 2 * LANES] = key_sum[...].astype(jnp.bfloat16)
        grads[:, 2 * LANES :] = value_sum[...].astype(jnp.bfloat16)

    return kernel


def attend_backward(packed, pair, key_side, kept, mixed, grad_mixed):
    length = packed.shape[0]
    whole = pl.BlockSpec((length, LANES), lambda g: (0, 0))
    return pl.pallas_call(
        backward_kernel(length, fitting_rows(length)),
        grid=(1,),
        in_specs=[pl.BlockSpec((length, LANES), lambda g, i=i: (0, 3 * pair + i)) for i in range(3)]
        + [whole, pl.BlockSpec((2, length, LANES), lambda g: (0, 0, 0)), whole, whole],
        out_specs=pl.BlockSpec((length, 3 * LANES), lambda g: (0, 0)),
        out_shape=jax.ShapeDtypeStruct((length, 3 * LANES), jnp.bfloat16),
        scratch_shapes=[pltpu.VMEM((length, LANES), jnp.float32)] * 2,
        cost_estimate=pl.CostEstimate(
            flops=2 * 2 * length * length * 900,
            transcendentals=2 * length * length,
            bytes_accessed=length * LANES * 2 * 11,
        ),
        name="attend_backward",
    )(packed, packed, packed, key_side, kept, mixed, grad_mixed)


def ring(axis, step):
    members = lax.axis_size(axis)
    return [(i, (i + step) % members) for i in range(members)]


def across(array, axis, bit):
    members = lax.axis_size(axis)
    return lax.ppermute(array, axis, [(i, i ^ bit) for i in range(members)])


def gather_rows(array):
    if lax.axis_size("fsdp") != 2:
        return lax.all_gather(array, "fsdp", axis=0, tiled=True)
    other = across(array, "fsdp", 1)
    me = lax.axis_index("fsdp")
    rows = array.shape[0]
    twice = jnp.concatenate([array, array], axis=0)
    return lax.dynamic_update_slice(
        twice, other, ((1 - me) * rows,) + (0,) * (array.ndim - 1)
    )


def line_gather(array):
    members = lax.axis_size("seq")
    me = lax.axis_index("seq")
    up = [(i, i + 1) for i in range(members - 1)]
    down = [(i + 1, i) for i in range(members - 1)]
    ups, downs = [array], [array]
    for _ in range(members - 1):
        ups.append(lax.ppermute(ups[-1], "seq", up))
        downs.append(lax.ppermute(downs[-1], "seq", down))
    return [array] + [
        jnp.where(me >= s, ups[s], downs[members - s]) for s in range(1, members)
    ]


def line_scatter_sum(parts):
    members = lax.axis_size("seq")
    me = lax.axis_index("seq")
    up = [(i, i + 1) for i in range(members - 1)]
    down = [(i + 1, i) for i in range(members - 1)]
    zero = jnp.zeros((), jnp.float32)
    rising, falling = None, None
    for distance in range(members - 1, 0, -1):
        add_up = jnp.where(
            me + distance < members, parts[members - distance].astype(jnp.float32), zero
        )
        add_down = jnp.where(me - distance >= 0, parts[distance].astype(jnp.float32), zero)
        if rising is not None:
            add_up = add_up + rising.astype(jnp.float32)
            add_down = add_down + falling.astype(jnp.float32)
        rising = lax.ppermute(add_up.astype(jnp.bfloat16), "seq", up)
        falling = lax.ppermute(add_down.astype(jnp.bfloat16), "seq", down)
    return rising.astype(jnp.float32) + falling.astype(jnp.float32)


def every_bit(axis):
    members = lax.axis_size(axis)
    return [(axis, 1 << k) for k in range(members.bit_length() - 1)]


def total_of(array):
    for axis, bit in every_bit("fsdp") + every_bit("dp") + every_bit("seq"):
        array = array + across(array, axis, bit)
    return array


def own_number(steps):
    number = 0
    for axis, bit in steps:
        number = number * 2 + jnp.where((lax.axis_index(axis) & bit) != 0, 1, 0)
    return number


def halve(keep, send, steps):
    for place, (axis, bit) in enumerate(steps):
        got = across(send, axis, bit).astype(jnp.float32)
        if place + 1 == len(steps):
            return (keep.astype(jnp.float32) + got).astype(jnp.bfloat16)
        half = keep.shape[0] // 2
        send = (keep[half:].astype(jnp.float32) + got[half:]).astype(jnp.bfloat16)
        keep = (keep[:half].astype(jnp.float32) + got[:half]).astype(jnp.bfloat16)


def double(block, steps):
    for axis, bit in reversed(steps[1:]):
        block = jnp.concatenate([block, across(block, axis, bit)], axis=0)
    return block, across(block, *steps[0])


def product_kernel(tables, own_left, other_left, own_right, other_right, out):
    out[0] = (
        matmul_left(own_left[...], own_right[...])
        + matmul_left(other_left[...], other_right[...])
    ).astype(jnp.bfloat16)


def block_products(tables, own_left, other_left, own_right, other_right, height, width):
    tokens = own_left.shape[0]
    count = tables.shape[1]
    return pl.pallas_call(
        product_kernel,
        grid_spec=pltpu.PrefetchScalarGridSpec(
            num_scalar_prefetch=1,
            grid=(count,),
            in_specs=[
                pl.BlockSpec((tokens, height), lambda j, t: (0, t[0, j])),
                pl.BlockSpec((tokens, height), lambda j, t: (0, t[1, j])),
                pl.BlockSpec((tokens, width), lambda j, t: (0, t[2, j])),
                pl.BlockSpec((tokens, width), lambda j, t: (0, t[2, j])),
            ],
            out_specs=pl.BlockSpec((1, height, width), lambda j, t: (j, 0, 0)),
        ),
        out_shape=jax.ShapeDtypeStruct((count, height, width), jnp.bfloat16),
        cost_estimate=pl.CostEstimate(
            flops=4 * tokens * count * height * width,
            transcendentals=0,
            bytes_accessed=count * (4 * tokens * (height + width) + 2 * height * width),
        ),
        name="block_products",
    )(tables, own_left, other_left, own_right, other_right)


def spread_kernel(order, low, high, out):
    half = pl.num_programs(0) // 2
    step = pl.program_id(0)

    @pl.when(step < half)
    def _():
        out[...] = low[0].astype(jnp.float32)

    @pl.when(step >= half)
    def _():
        out[...] = high[0].astype(jnp.float32)


def spread_blocks(number, low, high, across_count):
    half, height, width = low.shape
    count = 2 * half
    order = jnp.arange(count, dtype=jnp.int32) ^ number
    table = jnp.stack([order // across_count, order % across_count])
    return pl.pallas_call(
        spread_kernel,
        grid_spec=pltpu.PrefetchScalarGridSpec(
            num_scalar_prefetch=1,
            grid=(count,),
            in_specs=[
                pl.BlockSpec((1, height, width), lambda j, t: (jnp.minimum(j, half - 1), 0, 0)),
                pl.BlockSpec((1, height, width), lambda j, t: (jnp.maximum(j - half, 0), 0, 0)),
            ],
            out_specs=pl.BlockSpec((height, width), lambda j, t: (t[0, j], t[1, j])),
        ),
        out_shape=jax.ShapeDtypeStruct(
            (count // across_count * height, across_count * width), jnp.float32
        ),
        cost_estimate=pl.CostEstimate(
            flops=0, transcendentals=0, bytes_accessed=count * height * width * 6
        ),
        name="spread_blocks",
    )(table, low, high)


def plain_sum(left, right):
    part = lax.psum_scatter(
        matmul_left(left, right), "fsdp", scatter_dimension=0, tiled=True
    )
    return lax.psum(part.astype(jnp.bfloat16), ("dp", "seq")).astype(jnp.float32)


def blocks_of(rows, columns, count):
    down = 4
    while down > 1 and (rows % (down * LANES) or count % down):
        down //= 2
    if rows % (down * LANES) or columns % ((count // down) * LANES):
        return None
    return down, count // down


def summed_gradient(left, right, steps, left_block=None):
    groups = lax.axis_size("fsdp")
    rows, columns = left.shape[1] // groups, right.shape[1]
    count = 1 << len(steps)
    shape = blocks_of(rows, columns, count)
    if groups != 2 or shape is None:
        if left_block is not None:
            order = jnp.stack([left_block(i) for i in range(left.shape[1] // LANES)])
            tiles = left.reshape(left.shape[0], -1, LANES)
            left = jnp.take(tiles, order, axis=1).reshape(left.shape)
        return plain_sum(left, right)
    down, along = shape
    height, width = rows // down, columns // along
    me = lax.axis_index("fsdp")
    number = own_number(steps)
    order = jnp.arange(count, dtype=jnp.int32) ^ number
    if left_block is None:
        other_left = across(
            lax.dynamic_slice(left, (0, (1 - me) * rows), (left.shape[0], rows)), "fsdp", 1
        )
        own_table = me * down + order // along
        other_table = order // along
    else:
        other_left = across(left, "fsdp", 1)
        own_table = left_block(me * down + order // along)
        other_table = own_table
    other_right = across(right, "fsdp", 1)
    tables = jnp.stack([own_table, other_table, order % along]).astype(jnp.int32)
    half = count // 2
    send = block_products(
        tables[:, half:], left, other_left, right, other_right, height, width
    )
    keep = block_products(
        tables[:, :half], left, other_left, right, other_right, height, width
    )
    block = halve(keep, send, steps)
    low, high = double(block, steps)
    return spread_blocks(number, low, high, along)


def head_product_kernel(table, left, right, out):
    count, height, width = out.shape
    picked = jnp.concatenate(
        [left[:, pl.ds(pl.multiple_of(table[j] * height, LANES), height)] for j in range(count)],
        axis=1,
    )
    out[...] = (
        matmul_left(picked, right[...]).astype(jnp.bfloat16).reshape(count, height, width)
    )


def head_products(table, left, right, height):
    count = table.shape[0]
    tokens, width = right.shape
    return pl.pallas_call(
        head_product_kernel,
        grid_spec=pltpu.PrefetchScalarGridSpec(
            num_scalar_prefetch=1,
            grid=(1,),
            in_specs=[
                pl.BlockSpec(left.shape, lambda j, t: (0, 0)),
                pl.BlockSpec(right.shape, lambda j, t: (0, 0)),
            ],
            out_specs=pl.BlockSpec((count, height, width), lambda j, t: (0, 0, 0)),
        ),
        out_shape=jax.ShapeDtypeStruct((count, height, width), jnp.bfloat16),
        cost_estimate=pl.CostEstimate(
            flops=2 * tokens * count * height * width,
            transcendentals=0,
            bytes_accessed=2 * left.size + 2 * right.size + 2 * count * height * width,
        ),
        name="head_products",
    )(table, left, right)


def head_spread_kernel(table, low, high, *refs):
    half = pl.num_programs(0) // 2
    step = pl.program_id(0)
    outs = refs[-3:]

    def put(source):
        tile = source[0, 0].astype(jnp.float32)
        for i in range(3):
            outs[i][...] = tile[:, i * LANES : (i + 1) * LANES]

    @pl.when(step < half)
    def _():
        put(low)

    @pl.when(step >= half)
    def _():
        put(high)


def head_spread(row_table, column_table, low, high, columns, earlier):
    half, members, height, width = low.shape
    count = 2 * half
    table = jnp.concatenate([row_table, column_table]).astype(jnp.int32)
    out = jax.ShapeDtypeStruct((count * height, columns), jnp.float32)
    given = [] if earlier is None else list(earlier)
    return pl.pallas_call(
        head_spread_kernel,
        grid_spec=pltpu.PrefetchScalarGridSpec(
            num_scalar_prefetch=1,
            grid=(count, members),
            in_specs=[
                pl.BlockSpec(
                    (1, 1, height, width),
                    lambda j, s, t: (
                        jnp.minimum(j, half - 1),
                        jnp.where(j < half, s, members - 1),
                        0,
                        0,
                    ),
                ),
                pl.BlockSpec(
                    (1, 1, height, width),
                    lambda j, s, t: (jnp.maximum(j - half, 0), jnp.where(j < half, 0, s), 0, 0),
                ),
            ]
            + [pl.BlockSpec(memory_space=pl.ANY)] * len(given),
            out_specs=[
                pl.BlockSpec((height, LANES), lambda j, s, t: (t[j], t[count + s]))
            ]
            * 3,
        ),
        out_shape=[out] * 3,
        input_output_aliases={3 + i: i for i in range(len(given))},
        name="head_spread",
    )(table, low, high, *given)


def head_gradients(start_low, head_grads, steps_of):
    members = lax.axis_size("seq")
    pairs = len(head_grads)
    columns = members * pairs * LANES
    groups = lax.axis_size("fsdp")
    devices = groups * lax.axis_size("dp")
    height = start_low.shape[1] // devices
    me = lax.axis_index("seq")
    if groups != 2 or height % LANES:
        found = []
        for which in range(3):
            cut = slice(which * LANES, (which + 1) * LANES)
            right = jnp.concatenate([each[:, cut] for each in head_grads], axis=1)
            part = lax.psum_scatter(
                matmul_left(start_low, right), "fsdp", scatter_dimension=0, tiled=True
            )
            part = lax.psum(part.astype(jnp.bfloat16), "dp")
            found.append(
                lax.all_gather(part, "seq", axis=1, tiled=True).astype(jnp.float32)
            )
        return found
    outs = None
    rows_half = 1 << (len(steps_of[0]) - 1)
    for pair, right in enumerate(head_grads):
        steps = [("fsdp", 1)] + steps_of[pair % 2]
        number = own_number(steps)
        table = (jnp.arange(2 * rows_half * 2, dtype=jnp.int32) ^ number).astype(jnp.int32)
        half = table.shape[0] // 2
        send = head_products(table[half:], start_low, right, height)
        keep = head_products(table[:half], start_low, right, height)
        block = halve(keep, send, steps)
        gathered = jnp.concatenate(
            [block] + [lax.ppermute(block, "seq", ring("seq", s)) for s in range(1, members)],
            axis=0,
        )[None]
        low, high = double(gathered, steps[1:])
        row_table = jnp.arange(half, dtype=jnp.int32) ^ own_number(steps[1:])
        column_table = ((me - jnp.arange(members, dtype=jnp.int32)) % members) * pairs + pair
        outs = head_spread(row_table, column_table, low, high, columns, outs)
    return list(outs)


def local(
    inputs,
    doc_ids,
    timesteps,
    query_weight,
    query_bias,
    key_weight,
    value_weight,
    value_bias,
    out_weight,
    out_bias,
    first_gain,
    first_shift,
    inner_weight,
    inner_bias,
    outer_weight,
    outer_bias,
    second_gain,
    second_shift,
    time_weight,
    time_bias,
    cotangent,
):
    members = lax.axis_size("seq")
    groups = lax.axis_size("fsdp")
    me = lax.axis_index("seq")
    core = lax.axis_index("fsdp")
    tokens = inputs.shape[1]
    width = query_weight.shape[1] // members
    pairs = width // LANES
    rows = query_weight.shape[0]

    pieces = []
    cuts = [
        lax.dynamic_slice(each, (0, me * width), (rows, width))
        for each in (query_weight, key_weight, value_weight)
    ]
    for pair in range(pairs):
        pieces += [each[:, pair * LANES : (pair + 1) * LANES] for each in cuts]
    head_matrix = gather_rows(jnp.concatenate(pieces, axis=1))
    small = jnp.stack(
        [
            query_bias,
            value_bias,
            out_bias,
            first_gain,
            first_shift,
            outer_bias,
            second_gain,
            second_shift,
            time_bias,
        ]
    )
    if groups == 2:
        packed = jnp.concatenate([small, inner_bias.reshape(-1, rows)], axis=0)
        other = across(packed, "fsdp", 1)
        first, second = jnp.where(core == 0, packed, other), jnp.where(core == 0, other, packed)
        vectors = jnp.concatenate([first[:9], second[:9]], axis=1)
        inner_offset = jnp.concatenate([first[9:], second[9:]], axis=0).reshape(-1)
    else:
        vectors = lax.all_gather(small, "fsdp", axis=1, tiled=True)
        inner_offset = lax.all_gather(inner_bias, "fsdp", axis=0, tiled=True)
    vectors = vectors.astype(jnp.float32)
    inner_offset = inner_offset.astype(jnp.float32)
    (
        query_offset,
        value_offset,
        out_offset,
        first_scale,
        first_offset,
        outer_offset,
        second_scale,
        second_offset,
        time_offset,
    ) = [vectors[i] for i in range(9)]

    features = time_features(timesteps).astype(jnp.bfloat16)
    time_matrix = gather_rows(time_weight)
    embedded = matmul(features, time_matrix) + time_offset

    halves = 2 if tokens % 32 == 0 else 1
    cut = tokens // halves
    sent = [line_gather(inputs[0, i * cut : (i + 1) * cut]) for i in range(halves)]
    segments = jnp.concatenate(
        [doc_ids[0]]
        + [lax.ppermute(doc_ids[0], "seq", ring("seq", s)) for s in range(1, members)]
    )
    out_matrix = gather_rows(out_weight)
    inner_matrix = gather_rows(inner_weight)
    outer_matrix = gather_rows(outer_weight)
    out_rolled = lax.dynamic_slice(
        jnp.concatenate([out_matrix, out_matrix], axis=0), (me * width, 0), out_matrix.shape
    )
    out_rolled = jnp.swapaxes(out_rolled.reshape(members, pairs, LANES, D), 0, 1).reshape(D, D)

    start = inputs[0].astype(jnp.float32) + embedded
    start_low = jnp.concatenate(
        [
            (sent[i][s].astype(jnp.float32) + embedded).astype(jnp.bfloat16)
            for s in range(members)
            for i in range(halves)
        ],
        axis=0,
    )
    own_query_offset = lax.dynamic_slice(query_offset, (me * width,), (width,))
    own_value_offset = lax.dynamic_slice(value_offset, (me * width,), (width,))
    offsets = []
    for pair in range(pairs):
        span = slice(pair * LANES, (pair + 1) * LANES)
        offsets += [
            own_query_offset[span],
            jnp.zeros((LANES,), jnp.float32),
            own_value_offset[span],
        ]
    projected = (matmul(start_low, head_matrix) + jnp.concatenate(offsets)).astype(jnp.bfloat16)
    key_side, query_side = sides(segments)

    mixed_own, kept, arrived = [], [], []
    for pair in range(pairs):
        mixed_pair, kept_pair = attend_forward(projected, pair, key_side, query_side)
        mixed_own.append(mixed_pair)
        kept.append(kept_pair)
        arrived.append(mixed_pair[:tokens])
        for s in range(1, members):
            arrived.append(
                lax.ppermute(
                    mixed_pair[s * tokens : (s + 1) * tokens], "seq", ring("seq", -s)
                )
            )
    mixed = jnp.concatenate(arrived, axis=1)

    attended = matmul(mixed, out_rolled) + out_offset
    first_out, first_back = jax.vjp(normalize, start + attended, first_scale, first_offset)
    first_low = first_out.astype(jnp.bfloat16)
    inner = matmul(first_low, inner_matrix) + inner_offset
    activated, gelu_back = jax.vjp(exact_gelu, inner)
    activated_low = activated.astype(jnp.bfloat16)
    outer = matmul(activated_low, outer_matrix) + outer_offset
    result, second_back = jax.vjp(normalize, first_out + outer, second_scale, second_offset)
    grad_second, second_gain_grad, second_shift_grad = second_back(
        cotangent[0].astype(jnp.float32)
    )
    grad_outer = grad_second.astype(jnp.bfloat16)

    dp_bits, seq_bits = every_bit("dp"), every_bit("seq")
    steps_of = [dp_bits + seq_bits, dp_bits[::-1] + seq_bits]
    outer_weight_grad = summed_gradient(activated_low, grad_outer, steps_of[0])
    outer_bias_grad = jnp.sum(grad_outer.astype(jnp.float32), axis=0)
    grad_activated = matmul_right(grad_outer, outer_matrix)
    grad_inner = gelu_back(grad_activated)[0].astype(jnp.bfloat16)
    inner_weight_grad = summed_gradient(first_low, grad_inner, steps_of[1])
    inner_bias_grad = jnp.sum(grad_inner.astype(jnp.float32), axis=0)
    grad_first_out = grad_second + matmul_right(grad_inner, inner_matrix)
    grad_first, first_gain_grad, first_shift_grad = first_back(grad_first_out)
    grad_attended = grad_first.astype(jnp.bfloat16)

    grad_mixed = matmul_right(grad_attended, out_rolled).astype(jnp.bfloat16)

    def mixed_block(block):
        owner, pair = block // pairs, block % pairs
        return pair * members + (owner - me) % members

    out_weight_grad = summed_gradient(mixed, grad_attended, steps_of[0], mixed_block)
    out_bias_grad = jnp.sum(grad_attended.astype(jnp.float32), axis=0)
    early = total_of(
        jnp.concatenate(
            [
                inner_bias_grad,
                outer_bias_grad,
                second_gain_grad,
                second_shift_grad,
                out_bias_grad,
                first_gain_grad,
                first_shift_grad,
            ]
        ).reshape(-1, LANES)
    )

    head_grads = []
    for pair in range(pairs):
        came = []
        for s in range(members):
            place = (pair * members + s) * LANES
            piece = grad_mixed[:, place : place + LANES]
            came.append(piece if s == 0 else lax.ppermute(piece, "seq", ring("seq", s)))
        head_grads.append(
            attend_backward(
                projected, pair, key_side, kept[pair], mixed_own[pair], jnp.concatenate(came)
            )
        )
    query_weight_grad, key_weight_grad, value_weight_grad = head_gradients(
        start_low, head_grads, [dp_bits, dp_bits[::-1]]
    )
    all_head_grads = jnp.concatenate(head_grads, axis=1)
    start_parts = [
        matmul_right(all_head_grads[s * tokens : (s + 1) * tokens], head_matrix)
        for s in range(members)
    ]
    grad_start = grad_first + start_parts[0] + line_scatter_sum(start_parts)

    column_sums = jnp.sum(all_head_grads.astype(jnp.float32), axis=0)
    grad_embedded = jnp.sum(grad_first, axis=0) + lax.dot_general(
        column_sums[None],
        head_matrix.astype(jnp.float32),
        (((1,), (1,)), ((), ())),
        precision=lax.Precision.HIGHEST,
    ).reshape(-1)
    by_kind = column_sums.reshape(pairs, 3, LANES)
    sequences = lax.axis_size("dp") * groups
    here = lax.axis_index("dp") * groups + core
    slot = (jnp.arange(sequences) == here).astype(jnp.float32)[:, None]
    placed_sums = [
        lax.dynamic_update_slice(
            jnp.zeros((1, D), jnp.float32), by_kind[:, i].reshape(1, width), (0, me * width)
        )
        for i in (0, 2)
    ]
    step_row = jnp.where(
        (jnp.arange(D) == here) & (me == 0), timesteps[0].astype(jnp.float32), 0.0
    )[None]
    late = total_of(
        jnp.concatenate([slot * grad_embedded[None]] + placed_sums + [step_row], axis=0)
    )
    embedded_grads = late[:sequences]
    every_features = time_features(late[sequences + 2, :sequences]).astype(jnp.bfloat16)
    own_features = lax.dynamic_slice(
        every_features.astype(jnp.float32), (0, core * rows), (sequences, rows)
    )
    time_weight_grad = lax.dot_general(
        own_features,
        embedded_grads,
        (((0,), (0,)), ((), ())),
        precision=lax.Precision.HIGHEST,
    )

    def own_rows(vector):
        size = vector.shape[0] // groups
        return lax.dynamic_slice(vector, (core * size,), (size,))

    early = early.reshape(-1)
    hidden = inner_offset.shape[0]
    rest = [own_rows(early[hidden + i * D : hidden + (i + 1) * D]) for i in range(6)]
    return (
        result.astype(jnp.bfloat16)[None],
        grad_start.astype(jnp.bfloat16)[None],
        query_weight_grad,
        own_rows(late[sequences]),
        key_weight_grad,
        value_weight_grad,
        own_rows(late[sequences + 1]),
        out_weight_grad,
        rest[3],
        rest[4],
        rest[5],
        inner_weight_grad,
        own_rows(early[:hidden]),
        outer_weight_grad,
        rest[0],
        rest[1],
        rest[2],
        time_weight_grad,
        own_rows(jnp.sum(embedded_grads, axis=0)),
    )


def solution(mesh):
    placed = (
        P(("dp", "fsdp"), "seq", None),
        P(("dp", "fsdp"), "seq"),
        P(("dp", "fsdp")),
        P("fsdp", None),
        P("fsdp"),
        P("fsdp", None),
        P("fsdp", None),
        P("fsdp"),
        P("fsdp", None),
        P("fsdp"),
        P("fsdp"),
        P("fsdp"),
        P("fsdp", None),
        P("fsdp"),
        P("fsdp", None),
        P("fsdp"),
        P("fsdp"),
        P("fsdp"),
        P("fsdp", None),
        P("fsdp"),
        P(("dp", "fsdp"), "seq", None),
    )
    return jax.shard_map(
        local,
        mesh=mesh,
        in_specs=placed,
        out_specs=(
            P(("dp", "fsdp"), "seq", None),
            P(("dp", "fsdp"), "seq", None),
            P("fsdp", None),
            P("fsdp"),
            P("fsdp", None),
            P("fsdp", None),
            P("fsdp"),
            P("fsdp", None),
            P("fsdp"),
            P("fsdp"),
            P("fsdp"),
            P("fsdp", None),
            P("fsdp"),
            P("fsdp", None),
            P("fsdp"),
            P("fsdp"),
            P("fsdp"),
            P("fsdp", None),
            P("fsdp"),
        ),
        check_vma=False,
    )
```

```python
import math

import jax
import jax.numpy as jnp
import numpy as np
from jax import lax
from jax.experimental import pallas as pl
from jax.experimental.pallas import tpu as pltpu
from jax.sharding import PartitionSpec as P

D = 1024
DH = 64
LANES = 128
FAR = -1e30


epsilon = 1e-05


def time_features(steps_given):
    half = D // 2
    frequency = np.exp(-math.log(10000.0) * np.arange(half) / half).astype(np.float32)
    angles = steps_given.astype(jnp.float32)[:, None] * jnp.asarray(frequency)[None, :]
    return jnp.concatenate([jnp.sin(angles), jnp.cos(angles)], axis=1)


def normalize(values, gain, shift):
    center = values - jnp.mean(values, axis=-1, keepdims=True)
    spread = jnp.mean(center * center, axis=-1, keepdims=True)
    return center * lax.rsqrt(spread + epsilon) * gain + shift


def exact_gelu(values):
    return jax.nn.gelu(values, approximate=False)


def matmul(left, right):
    return lax.dot_general(
        left, right, (((1,), (0,)), ((), ())), preferred_element_type=jnp.float32
    )


def matmul_left(left, right):
    return lax.dot_general(
        left, right, (((0,), (0,)), ((), ())), preferred_element_type=jnp.float32
    )


def matmul_right(left, right):
    return lax.dot_general(
        left, right, (((1,), (1,)), ((), ())), preferred_element_type=jnp.float32
    )


def sides(segments):
    length = segments.shape[0]
    lane = lax.broadcasted_iota(jnp.int32, (length, LANES), 1)
    same = segments[:, None] == lane
    key_side = jnp.where(
        lane < 8, jnp.where(same, 0.0, FAR), jnp.where(lane < 11, 1.0, 0.0)
    ).astype(jnp.bfloat16)
    query_side = jnp.where((lane < 8) & same, 1.0, 0.0).astype(jnp.bfloat16)
    return key_side, query_side


def placed_offset(column, lane, base):
    high = column.astype(jnp.bfloat16).astype(jnp.float32)
    rest = column - high
    middle = rest.astype(jnp.bfloat16).astype(jnp.float32)
    low = rest - middle
    return jnp.where(
        lane == 8, -high, jnp.where(lane == 9, -middle, jnp.where(lane == 10, -low, base))
    )


def forward_kernel(length, rows):
    def kernel(query, keys, values, key_side, query_side, mixed, kept):
        lane = lax.broadcasted_iota(jnp.int32, (rows, LANES), 1)
        wide_keys = jnp.concatenate([keys[...], key_side[...]], axis=1)
        all_values = values[...]
        for step in range(length // rows):
            part = pl.ds(step * rows, rows)
            pair = query[part, :] * jnp.bfloat16(0.125)
            side = query_side[part, :]
            outs = []
            for head in range(2):
                mine = (lane < DH) if head == 0 else (lane >= DH)
                wide = jnp.concatenate([jnp.where(mine, pair, jnp.bfloat16(0)), side], axis=1)
                scores = matmul_right(wide, wide_keys)
                top = jnp.max(scores, axis=1, keepdims=True)
                expon = jnp.exp(scores - top)
                total = jnp.sum(expon, axis=1, keepdims=True)
                shares = (expon * (1.0 / total)).astype(jnp.bfloat16)
                outs.append(matmul(shares, all_values))
                kept[head, part, :] = placed_offset(
                    top + jnp.log(total), lane, side.astype(jnp.float32)
                ).astype(jnp.bfloat16)
            mixed[part, :] = jnp.where(lane < DH, outs[0], outs[1]).astype(jnp.bfloat16)

    return kernel


def fitting_rows(length):
    for rows in (512, 384, 256, 128):
        if length % rows == 0:
            return rows
    return length


def attend_forward(packed, pair, key_side, query_side):
    length = packed.shape[0]
    whole = pl.BlockSpec((length, LANES), lambda g: (0, 0))
    return pl.pallas_call(
        forward_kernel(length, fitting_rows(length)),
        grid=(1,),
        in_specs=[pl.BlockSpec((length, LANES), lambda g, i=i: (0, 3 * pair + i)) for i in range(3)]
        + [whole, whole],
        out_specs=[whole, pl.BlockSpec((2, length, LANES), lambda g: (0, 0, 0))],
        out_shape=[
            jax.ShapeDtypeStruct((length, LANES), jnp.bfloat16),
            jax.ShapeDtypeStruct((2, length, LANES), jnp.bfloat16),
        ],
        cost_estimate=pl.CostEstimate(
            flops=2 * 2 * length * length * 384,
            transcendentals=2 * length * length,
            bytes_accessed=length * LANES * 2 * 8,
        ),
        name="attend_forward",
    )(packed, packed, packed, key_side, query_side)


def backward_kernel(length, rows):
    def kernel(
        query, keys, values, key_side, kept, mixed, grad_mixed, grads, key_sum, value_sum
    ):
        lane = lax.broadcasted_iota(jnp.int32, (rows, LANES), 1)
        wide_keys = jnp.concatenate([keys[...], key_side[...]], axis=1)
        wide_values = jnp.concatenate([values[...], key_side[...]], axis=1)
        all_keys = keys[...]
        for step in range(length // rows):
            part = pl.ds(step * rows, rows)
            pair = query[part, :] * jnp.bfloat16(0.125)
            grad = grad_mixed[part, :]
            product = grad.astype(jnp.float32) * mixed[part, :].astype(jnp.float32)
            outs = []
            for head in range(2):
                mine = (lane < DH) if head == 0 else (lane >= DH)
                own_query = jnp.where(mine, pair, jnp.bfloat16(0))
                own_grad = jnp.where(mine, grad, jnp.bfloat16(0))
                centered = jnp.sum(jnp.where(mine, product, 0.0), axis=1, keepdims=True)
                side = placed_offset(centered, lane, 0.0).astype(jnp.bfloat16)
                scores = matmul_right(
                    wide_keys, jnp.concatenate([own_query, kept[head, part, :]], axis=1)
                )
                shares = jnp.exp(scores)
                share_grad = matmul_right(
                    wide_values, jnp.concatenate([own_grad, side], axis=1)
                )
                score_grad = (shares * share_grad).astype(jnp.bfloat16)
                low_shares = shares.astype(jnp.bfloat16)
                key_part = matmul(score_grad, own_query)
                value_part = matmul(low_shares, own_grad)
                if step == 0 and head == 0:
                    key_sum[...] = key_part
                    value_sum[...] = value_part
                else:
                    key_sum[...] += key_part
                    value_sum[...] += value_part
                outs.append(matmul_left(score_grad, all_keys))
            grads[part, :LANES] = (jnp.where(lane < DH, outs[0], outs[1]) * 0.125).astype(
                jnp.bfloat16
            )
        grads[:, LANES : 2 * LANES] = key_sum[...].astype(jnp.bfloat16)
        grads[:, 2 * LANES :] = value_sum[...].astype(jnp.bfloat16)

    return kernel


def attend_backward(packed, pair, key_side, kept, mixed, grad_mixed):
    length = packed.shape[0]
    whole = pl.BlockSpec((length, LANES), lambda g: (0, 0))
    return pl.pallas_call(
        backward_kernel(length, fitting_rows(length)),
        grid=(1,),
        in_specs=[pl.BlockSpec((length, LANES), lambda g, i=i: (0, 3 * pair + i)) for i in range(3)]
        + [whole, pl.BlockSpec((2, length, LANES), lambda g: (0, 0, 0)), whole, whole],
        out_specs=pl.BlockSpec((length, 3 * LANES), lambda g: (0, 0)),
        out_shape=jax.ShapeDtypeStruct((length, 3 * LANES), jnp.bfloat16),
        scratch_shapes=[pltpu.VMEM((length, LANES), jnp.float32)] * 2,
        cost_estimate=pl.CostEstimate(
            flops=2 * 2 * length * length * 900,
            transcendentals=2 * length * length,
            bytes_accessed=length * LANES * 2 * 11,
        ),
        name="attend_backward",
    )(packed, packed, packed, key_side, kept, mixed, grad_mixed)


def across(array, axis, bit, name):
    members = lax.axis_size(axis)
    with jax.named_scope(name):
        return lax.ppermute(array, axis, [(i, i ^ bit) for i in range(members)])


def join_kernel(table, own, other, out):
    half = pl.num_programs(0) // 2
    step = pl.program_id(0)

    @pl.when(step < half)
    def _():
        out[...] = own[...]

    @pl.when(step >= half)
    def _():
        out[...] = other[...]


def gather_rows(array, name):
    if lax.axis_size("fsdp") != 2:
        return lax.all_gather(array, "fsdp", axis=0, tiled=True)
    other = across(array, "fsdp", 1, name)
    me = lax.axis_index("fsdp")
    rows, columns = array.shape
    steps = max(1, rows * columns // (512 * 1024))
    block = (rows // steps, columns)
    with jax.named_scope(name + "_join"):
        return pl.pallas_call(
            join_kernel,
            grid_spec=pltpu.PrefetchScalarGridSpec(
                num_scalar_prefetch=1,
                grid=(2 * steps,),
                in_specs=[
                    pl.BlockSpec(block, lambda i, t: (jnp.minimum(i, steps - 1), 0)),
                    pl.BlockSpec(block, lambda i, t: (jnp.maximum(i - steps, 0), 0)),
                ],
                out_specs=pl.BlockSpec(
                    block,
                    lambda i, t: (
                        jnp.where(i < steps, t[0] * steps + i, (1 - t[0]) * steps + i - steps),
                        0,
                    ),
                ),
            ),
            out_shape=jax.ShapeDtypeStruct((2 * rows, columns), array.dtype),
            cost_estimate=pl.CostEstimate(
                flops=0, transcendentals=0, bytes_accessed=8 * rows * columns
            ),
            name="join_rows",
        )(me[None], array, other)


def seq_gather(array):
    members = lax.axis_size("seq")
    if members != 4:
        return [array] + [across(array, "seq", s, "tokens") for s in range(1, members)]
    me = lax.axis_index("seq")

    def sent(value, pairs, name):
        with jax.named_scope(name):
            return lax.ppermute(value, "seq", pairs)

    middle, outward = [(1, 2), (2, 1)], [(1, 0), (2, 3)]
    near = across(array, "seq", 1, "tokens_near")
    far = sent(array, middle, "tokens_far")
    further = sent(near, middle, "tokens_further")
    end = sent(far, outward, "tokens_end")
    last = sent(further, outward, "tokens_last")
    between = (me == 1) | (me == 2)
    return [array, near, jnp.where(between, further, end), jnp.where(between, far, last)]


def every_bit(axis):
    members = lax.axis_size(axis)
    return [(axis, 1 << k) for k in range(members.bit_length() - 1)]


def total_of(array):
    for axis, bit in every_bit("fsdp") + every_bit("dp") + every_bit("seq"):
        array = array + across(array, axis, bit, f"vectors_{axis}{bit}")
    return array


def own_number(steps):
    number = 0
    for axis, bit in steps:
        number = number * 2 + jnp.where((lax.axis_index(axis) & bit) != 0, 1, 0)
    return number


def halve(keep, send, steps, name):
    for place, (axis, bit) in enumerate(steps):
        got = across(send, axis, bit, f"{name}_rs{place}")
        if place + 1 == len(steps):
            return keep + got
        half = keep.shape[0] // 2
        send = keep[half:] + got[half:]
        keep = keep[:half] + got[:half]


def double(block, steps, name):
    for place in range(len(steps) - 1, 0, -1):
        block = jnp.concatenate(
            [block, across(block, *steps[place], f"{name}_ag{place}")], axis=0
        )
    return block, across(block, *steps[0], f"{name}_ag0")


GROUP = 4


def product_kernel(tables, own_left, other_left, own_right, other_right, out):
    left = jnp.concatenate([own_left[...], other_left[...]], axis=0)
    right = jnp.concatenate([own_right[...], other_right[...]], axis=0)
    product = matmul_left(left, right).astype(jnp.bfloat16)
    width = out.shape[2]
    for i in range(GROUP):
        out[i ^ tables[4, 0]] = product[:, i * width : (i + 1) * width]


def block_products(tables, own_left, other_left, own_right, other_right, height, width):
    tokens = own_left.shape[0]
    count = tables.shape[1]
    return pl.pallas_call(
        product_kernel,
        grid_spec=pltpu.PrefetchScalarGridSpec(
            num_scalar_prefetch=1,
            grid=(count,),
            in_specs=[
                pl.BlockSpec((tokens, height), lambda j, t: (0, t[0, j])),
                pl.BlockSpec((tokens, height), lambda j, t: (0, t[1, j])),
                pl.BlockSpec((tokens, GROUP * width), lambda j, t: (0, t[2, j])),
                pl.BlockSpec((tokens, GROUP * width), lambda j, t: (0, t[2, j])),
            ],
            out_specs=pl.BlockSpec((GROUP, height, width), lambda j, t: (j, 0, 0)),
        ),
        out_shape=jax.ShapeDtypeStruct((GROUP * count, height, width), jnp.bfloat16),
        cost_estimate=pl.CostEstimate(
            flops=4 * tokens * count * GROUP * height * width,
            transcendentals=0,
            bytes_accessed=count * (4 * tokens * (height + GROUP * width) + 8 * height * width),
        ),
        name="block_products",
    )(tables, own_left, other_left, own_right, other_right)


def spread_kernel(table, low, high, out):
    half = pl.num_programs(0) // 2
    step = pl.program_id(0)
    width = low.shape[2]

    def put(source):
        for i in range(GROUP):
            place = pl.multiple_of((i ^ table[2, 0]) * width, LANES)
            out[:, pl.ds(place, width)] = source[i].astype(jnp.float32)

    @pl.when(step < half)
    def _():
        put(low)

    @pl.when(step >= half)
    def _():
        put(high)


def spread_blocks(number, low, high, along):
    half, height, width = low.shape
    groups = 2 * half // GROUP
    order = jnp.arange(groups, dtype=jnp.int32) ^ (number // GROUP)
    each = along // GROUP
    table = jnp.stack([order // each, order % each, jnp.full_like(order, number % GROUP)])
    last = groups // 2
    return pl.pallas_call(
        spread_kernel,
        grid_spec=pltpu.PrefetchScalarGridSpec(
            num_scalar_prefetch=1,
            grid=(groups,),
            in_specs=[
                pl.BlockSpec(
                    (GROUP, height, width), lambda j, t: (jnp.minimum(j, last - 1), 0, 0)
                ),
                pl.BlockSpec(
                    (GROUP, height, width), lambda j, t: (jnp.maximum(j - last, 0), 0, 0)
                ),
            ],
            out_specs=pl.BlockSpec((height, GROUP * width), lambda j, t: (t[0, j], t[1, j])),
        ),
        out_shape=jax.ShapeDtypeStruct(
            (2 * half // along * height, along * width), jnp.float32
        ),
        cost_estimate=pl.CostEstimate(
            flops=0, transcendentals=0, bytes_accessed=2 * half * height * width * 6
        ),
        name="spread_blocks",
    )(table, low, high)


def plain_sum(left, right):
    part = lax.psum_scatter(
        matmul_left(left, right), "fsdp", scatter_dimension=0, tiled=True
    )
    return lax.psum(part.astype(jnp.bfloat16), ("dp", "seq")).astype(jnp.float32)


def blocks_of(rows, columns, count, down):
    if count % (2 * GROUP) or rows % (down * LANES) or count % (down * GROUP):
        return None
    along = count // down
    if columns % (along * LANES):
        return None
    return down, along


def summed_gradient(left, right, steps, down, name, left_block=None):
    groups = lax.axis_size("fsdp")
    rows, columns = left.shape[1] // groups, right.shape[1]
    count = 1 << len(steps)
    shape = blocks_of(rows, columns, count, down)
    if groups != 2 or shape is None:
        if left_block is not None:
            order = jnp.stack([left_block(i) for i in range(left.shape[1] // LANES)])
            tiles = left.reshape(left.shape[0], -1, LANES)
            left = jnp.take(tiles, order, axis=1).reshape(left.shape)
        return plain_sum(left, right)
    down, along = shape
    height, width = rows // down, columns // along
    me = lax.axis_index("fsdp")
    number = own_number(steps)
    order = jnp.arange(count // GROUP, dtype=jnp.int32) ^ (number // GROUP)
    each = along // GROUP
    if left_block is None:
        other_left = across(
            lax.dynamic_slice(left, (0, (1 - me) * rows), (left.shape[0], rows)),
            "fsdp",
            1,
            f"{name}_left",
        )
        own_table = me * down + order // each
        other_table = order // each
    else:
        other_left = across(left, "fsdp", 1, f"{name}_left")
        own_table = left_block(me * down + order // each)
        other_table = own_table
    other_right = across(right, "fsdp", 1, f"{name}_right")
    low = jnp.full_like(order, number % GROUP)
    tables = jnp.stack([own_table, other_table, order % each, order, low]).astype(jnp.int32)
    half = count // GROUP // 2
    with jax.named_scope(f"{name}_send"):
        send = block_products(
            tables[:, half:], left, other_left, right, other_right, height, width
        )
    with jax.named_scope(f"{name}_keep"):
        keep = block_products(
            tables[:, :half], left, other_left, right, other_right, height, width
        )
    block = halve(keep, send, steps, name)
    low, high = double(block, steps, name)
    with jax.named_scope(f"{name}_spread"):
        return spread_blocks(number, low, high, along)


def head_product_kernel(table, left, right, keep, send):
    count, height, width = keep.shape
    for out, begin in ((send, count), (keep, 0)):
        picked = jnp.concatenate(
            [
                left[:, pl.ds(pl.multiple_of(table[begin + j] * height, LANES), height)]
                for j in range(count)
            ],
            axis=1,
        )
        out[...] = (
            matmul_left(picked, right[...]).astype(jnp.bfloat16).reshape(count, height, width)
        )


def head_products(table, left, right, height):
    half = table.shape[0] // 2
    tokens, width = right.shape
    out = jax.ShapeDtypeStruct((half, height, width), jnp.bfloat16)
    return pl.pallas_call(
        head_product_kernel,
        grid_spec=pltpu.PrefetchScalarGridSpec(
            num_scalar_prefetch=1,
            grid=(1,),
            in_specs=[
                pl.BlockSpec(left.shape, lambda j, t: (0, 0)),
                pl.BlockSpec(right.shape, lambda j, t: (0, 0)),
            ],
            out_specs=[pl.BlockSpec((half, height, width), lambda j, t: (0, 0, 0))] * 2,
        ),
        out_shape=[out, out],
        cost_estimate=pl.CostEstimate(
            flops=4 * tokens * half * height * width,
            transcendentals=0,
            bytes_accessed=2 * left.size + 2 * right.size + 4 * half * height * width,
        ),
        name="head_products",
    )(table, left, right)


def head_spread_kernel(pairs, members, half):
    def kernel(table, *refs):
        outs = refs[2 * pairs :]
        step = pl.program_id(0)
        count = pl.num_programs(0)

        def put(source, pair):
            for s in range(members):
                column = table[pairs * count + s] * pairs + pair
                place = pl.multiple_of(column * LANES, LANES)
                tile = source[0, s].astype(jnp.float32)
                for i in range(3):
                    outs[i][:, pl.ds(place, LANES)] = tile[:, i * LANES : (i + 1) * LANES]

        for pair in range(pairs):
            found = table[pair * count + step]

            @pl.when(found < half)
            def _():
                put(refs[2 * pair], pair)

            @pl.when(found >= half)
            def _():
                put(refs[2 * pair + 1], pair)

    return kernel


def head_spread(tables, parts, columns):
    pairs = len(parts)
    half, members, height, width = parts[0][0].shape
    count = 2 * half
    specs = []
    for pair in range(pairs):
        specs += [
            pl.BlockSpec(
                (1, members, height, width),
                lambda j, t, p=pair: (jnp.minimum(t[p * count + j], half - 1), 0, 0, 0),
            ),
            pl.BlockSpec(
                (1, members, height, width),
                lambda j, t, p=pair: (jnp.maximum(t[p * count + j] - half, 0), 0, 0, 0),
            ),
        ]
    return pl.pallas_call(
        head_spread_kernel(pairs, members, half),
        grid_spec=pltpu.PrefetchScalarGridSpec(
            num_scalar_prefetch=1,
            grid=(count,),
            in_specs=specs,
            out_specs=[pl.BlockSpec((height, columns), lambda j, t: (j, 0))] * 3,
        ),
        out_shape=[jax.ShapeDtypeStruct((count * height, columns), jnp.float32)] * 3,
        cost_estimate=pl.CostEstimate(
            flops=0, transcendentals=0, bytes_accessed=count * height * columns * 18
        ),
        name="head_spread",
    )(tables.astype(jnp.int32), *[each for part in parts for each in part])


def head_gradients(start_low, head_grads, steps_of):
    members = lax.axis_size("seq")
    pairs = len(head_grads)
    columns = members * pairs * LANES
    groups = lax.axis_size("fsdp")
    devices = groups * lax.axis_size("dp")
    height = start_low.shape[1] // devices
    me = lax.axis_index("seq")
    if groups != 2 or height % LANES:
        found = []
        for which in range(3):
            cut = slice(which * LANES, (which + 1) * LANES)
            right = jnp.concatenate([each[:, cut] for each in head_grads], axis=1)
            part = lax.psum_scatter(
                matmul_left(start_low, right), "fsdp", scatter_dimension=0, tiled=True
            )
            part = lax.psum(part.astype(jnp.bfloat16), "dp")
            found.append(
                lax.all_gather(part, "seq", axis=1, tiled=True).astype(jnp.float32)
            )
        return found
    parts, tables = [], []
    for pair, right in enumerate(head_grads):
        name = f"head{pair}"
        steps = [("fsdp", 1)] + steps_of[pair % 2]
        number = own_number(steps)
        table = jnp.arange(devices, dtype=jnp.int32) ^ number
        with jax.named_scope(f"{name}_products"):
            keep, send = head_products(table, start_low, right, height)
        block = halve(keep, send, steps, name)
        gathered = jnp.concatenate(
            [block] + [across(block, "seq", s, f"{name}_seq{s}") for s in range(1, members)],
            axis=0,
        )[None]
        parts.append(double(gathered, steps[1:], name))
        tables.append(
            jnp.arange(devices // groups, dtype=jnp.int32) ^ own_number(steps[1:])
        )
    tables.append(me ^ jnp.arange(members, dtype=jnp.int32))
    with jax.named_scope("head_spread"):
        return list(head_spread(jnp.concatenate(tables), parts, columns))


def local(
    inputs,
    doc_ids,
    timesteps,
    query_weight,
    query_bias,
    key_weight,
    value_weight,
    value_bias,
    out_weight,
    out_bias,
    first_gain,
    first_shift,
    inner_weight,
    inner_bias,
    outer_weight,
    outer_bias,
    second_gain,
    second_shift,
    time_weight,
    time_bias,
    cotangent,
):
    members = lax.axis_size("seq")
    groups = lax.axis_size("fsdp")
    me = lax.axis_index("seq")
    core = lax.axis_index("fsdp")
    tokens = inputs.shape[1]
    width = query_weight.shape[1] // members
    pairs = width // LANES
    rows = query_weight.shape[0]

    sent = seq_gather(inputs[0])
    segments = jnp.concatenate(
        [doc_ids[0]] + [across(doc_ids[0], "seq", s, "documents") for s in range(1, members)]
    )

    def own_heads(place):
        cuts = [
            lax.dynamic_slice(each, (0, (me ^ place) * width), (rows, width))
            for each in (query_weight, key_weight, value_weight)
        ]
        return [
            each[:, pair * LANES : (pair + 1) * LANES] for pair in range(pairs) for each in cuts
        ]

    head_matrix = gather_rows(jnp.concatenate(own_heads(0), axis=1), "head_weight")
    small = jnp.stack(
        [
            query_bias,
            value_bias,
            out_bias,
            first_gain,
            first_shift,
            outer_bias,
            second_gain,
            second_shift,
            time_bias,
        ]
    )
    if groups == 2:
        packed = jnp.concatenate([small, inner_bias.reshape(-1, rows)], axis=0)
        other = across(packed, "fsdp", 1, "small")
        first, second = jnp.where(core == 0, packed, other), jnp.where(core == 0, other, packed)
        vectors = jnp.concatenate([first[:9], second[:9]], axis=1)
        inner_offset = jnp.concatenate([first[9:], second[9:]], axis=0).reshape(-1)
    else:
        vectors = lax.all_gather(small, "fsdp", axis=1, tiled=True)
        inner_offset = lax.all_gather(inner_bias, "fsdp", axis=0, tiled=True)
    vectors = vectors.astype(jnp.float32)
    inner_offset = inner_offset.astype(jnp.float32)
    (
        query_offset,
        value_offset,
        out_offset,
        first_scale,
        first_offset,
        outer_offset,
        second_scale,
        second_offset,
        time_offset,
    ) = [vectors[i] for i in range(9)]

    features = time_features(timesteps).astype(jnp.bfloat16)
    time_matrix = gather_rows(time_weight, "time_weight")
    embedded = matmul(features, time_matrix) + time_offset

    out_matrix = gather_rows(out_weight, "out_weight")
    inner_matrix = gather_rows(inner_weight, "inner_weight")
    outer_matrix = gather_rows(outer_weight, "outer_weight")
    by_member = [
        lax.dynamic_slice(out_matrix, ((me ^ s) * width, 0), (width, D)) for s in range(members)
    ]
    out_rolled = jnp.concatenate(
        [
            each[pair * LANES : (pair + 1) * LANES]
            for pair in range(pairs)
            for each in by_member
        ],
        axis=0,
    )

    start = inputs[0].astype(jnp.float32) + embedded
    start_low = jnp.concatenate(
        [(sent[s].astype(jnp.float32) + embedded).astype(jnp.bfloat16) for s in range(members)],
        axis=0,
    )
    own_query_offset = lax.dynamic_slice(query_offset, (me * width,), (width,))
    own_value_offset = lax.dynamic_slice(value_offset, (me * width,), (width,))
    offsets = []
    for pair in range(pairs):
        span = slice(pair * LANES, (pair + 1) * LANES)
        offsets += [
            own_query_offset[span],
            jnp.zeros((LANES,), jnp.float32),
            own_value_offset[span],
        ]
    projected = (matmul(start_low, head_matrix) + jnp.concatenate(offsets)).astype(jnp.bfloat16)
    key_side, query_side = sides(segments)

    mixed_own, kept, arrived = [], [], []
    for pair in range(pairs):
        with jax.named_scope(f"attend_f{pair}"):
            mixed_pair, kept_pair = attend_forward(projected, pair, key_side, query_side)
        mixed_own.append(mixed_pair)
        kept.append(kept_pair)
        arrived.append(mixed_pair[:tokens])
        for s in range(1, members):
            arrived.append(
                across(mixed_pair[s * tokens : (s + 1) * tokens], "seq", s, f"mixed{pair}_{s}")
            )
    mixed = jnp.concatenate(arrived, axis=1)

    every_head = jnp.concatenate([each for s in range(members) for each in own_heads(s)], axis=1)

    attended = matmul(mixed, out_rolled) + out_offset
    first_out, first_back = jax.vjp(normalize, start + attended, first_scale, first_offset)
    first_low = first_out.astype(jnp.bfloat16)
    inner = matmul(first_low, inner_matrix) + inner_offset
    below = 0.5 * (1.0 + lax.erf(inner * np.float32(math.sqrt(0.5))))
    activated_low = (inner * below).astype(jnp.bfloat16)
    outer = matmul(activated_low, outer_matrix) + outer_offset
    result, second_back = jax.vjp(normalize, first_out + outer, second_scale, second_offset)
    grad_second, second_gain_grad, second_shift_grad = second_back(
        cotangent[0].astype(jnp.float32)
    )
    grad_outer = grad_second.astype(jnp.bfloat16)

    dp_bits, seq_bits = every_bit("dp"), every_bit("seq")
    steps_of = [dp_bits + seq_bits, dp_bits[::-1] + seq_bits]
    outer_weight_grad = summed_gradient(activated_low, grad_outer, steps_of[0], 4, "outer")
    outer_bias_grad = jnp.sum(grad_outer.astype(jnp.float32), axis=0)
    grad_activated = matmul_right(grad_outer, outer_matrix)
    slope = below + inner * (
        jnp.exp(-0.5 * inner * inner) * np.float32(1.0 / math.sqrt(2.0 * math.pi))
    )
    grad_inner = (grad_activated * slope).astype(jnp.bfloat16)
    inner_weight_grad = summed_gradient(first_low, grad_inner, steps_of[1], 1, "inner")
    inner_bias_grad = jnp.sum(grad_inner.astype(jnp.float32), axis=0)
    grad_first_out = grad_second + matmul_right(grad_inner, inner_matrix)
    grad_first, first_gain_grad, first_shift_grad = first_back(grad_first_out)
    grad_attended = grad_first.astype(jnp.bfloat16)

    grad_mixed = matmul_right(grad_attended, out_rolled).astype(jnp.bfloat16)

    def mixed_block(block):
        owner, pair = block // pairs, block % pairs
        return pair * members + (owner ^ me)

    out_weight_grad = summed_gradient(
        mixed, grad_attended, seq_bits + dp_bits, 4, "out", mixed_block
    )
    out_bias_grad = jnp.sum(grad_attended.astype(jnp.float32), axis=0)

    head_grads, returned = [], [[] for _ in range(members)]
    for pair in range(pairs):
        came = []
        for s in range(members):
            place = (pair * members + s) * LANES
            piece = grad_mixed[:, place : place + LANES]
            came.append(piece if s == 0 else across(piece, "seq", s, f"gmixed{pair}_{s}"))
        with jax.named_scope(f"attend_b{pair}"):
            grads = attend_backward(
                projected, pair, key_side, kept[pair], mixed_own[pair], jnp.concatenate(came)
            )
        head_grads.append(grads)
        for s in range(members):
            piece = grads[s * tokens : (s + 1) * tokens]
            returned[s].append(piece if s == 0 else across(piece, "seq", s, f"ghead{pair}_{s}"))
    query_weight_grad, key_weight_grad, value_weight_grad = head_gradients(
        start_low, head_grads, [dp_bits, dp_bits[::-1]]
    )
    all_returned = jnp.concatenate([each for place in returned for each in place], axis=1)
    if groups == 2:
        other_heads = across(every_head, "fsdp", 1, "every_head")
        own_part = matmul_right(all_returned, every_head)
        other_part = matmul_right(all_returned, other_heads)
        through_heads = jnp.where(
            core == 0,
            jnp.concatenate([own_part, other_part], axis=1),
            jnp.concatenate([other_part, own_part], axis=1),
        )
    else:
        through_heads = matmul_right(
            all_returned, lax.all_gather(every_head, "fsdp", axis=0, tiled=True)
        )
    grad_start = grad_first + through_heads

    column_sums = jnp.concatenate(
        [jnp.sum(each.astype(jnp.float32), axis=0) for each in head_grads]
    )
    grad_embedded = jnp.sum(grad_first, axis=0) + lax.dot_general(
        column_sums[None],
        head_matrix.astype(jnp.float32),
        (((1,), (1,)), ((), ())),
        precision=lax.Precision.HIGHEST,
    ).reshape(-1)
    by_kind = column_sums.reshape(pairs, 3, LANES)
    sequences = lax.axis_size("dp") * groups
    here = lax.axis_index("dp") * groups + core
    slot = (jnp.arange(sequences) == here).astype(jnp.float32)[:, None]
    placed_sums = [
        lax.dynamic_update_slice(
            jnp.zeros((1, D), jnp.float32), by_kind[:, i].reshape(1, width), (0, me * width)
        )
        for i in (0, 2)
    ]
    step_row = jnp.where(
        (jnp.arange(D) == here) & (me == 0), timesteps[0].astype(jnp.float32), 0.0
    )[None]
    hidden = inner_offset.shape[0]
    sums = total_of(
        jnp.concatenate(
            [
                slot * grad_embedded[None],
                *placed_sums,
                step_row,
                outer_bias_grad[None],
                second_gain_grad[None],
                second_shift_grad[None],
                out_bias_grad[None],
                first_gain_grad[None],
                first_shift_grad[None],
                inner_bias_grad.reshape(-1, D),
            ],
            axis=0,
        )
    )
    embedded_grads = sums[:sequences]
    every_features = time_features(sums[sequences + 2, :sequences]).astype(jnp.bfloat16)
    own_features = lax.dynamic_slice(
        every_features.astype(jnp.float32), (0, core * rows), (sequences, rows)
    )
    time_weight_grad = lax.dot_general(
        own_features,
        embedded_grads,
        (((0,), (0,)), ((), ())),
        precision=lax.Precision.HIGHEST,
    )

    def own_rows(vector):
        size = vector.shape[0] // groups
        return lax.dynamic_slice(vector, (core * size,), (size,))

    rest = [own_rows(sums[sequences + 3 + i]) for i in range(6)]
    return (
        result.astype(jnp.bfloat16)[None],
        grad_start.astype(jnp.bfloat16)[None],
        query_weight_grad,
        own_rows(sums[sequences]),
        key_weight_grad,
        value_weight_grad,
        own_rows(sums[sequences + 1]),
        out_weight_grad,
        rest[3],
        rest[4],
        rest[5],
        inner_weight_grad,
        own_rows(sums[sequences + 9 :].reshape(hidden)),
        outer_weight_grad,
        rest[0],
        rest[1],
        rest[2],
        time_weight_grad,
        own_rows(jnp.sum(embedded_grads, axis=0)),
    )


def solution(mesh):
    placed = (
        P(("dp", "fsdp"), "seq", None),
        P(("dp", "fsdp"), "seq"),
        P(("dp", "fsdp")),
        P("fsdp", None),
        P("fsdp"),
        P("fsdp", None),
        P("fsdp", None),
        P("fsdp"),
        P("fsdp", None),
        P("fsdp"),
        P("fsdp"),
        P("fsdp"),
        P("fsdp", None),
        P("fsdp"),
        P("fsdp", None),
        P("fsdp"),
        P("fsdp"),
        P("fsdp"),
        P("fsdp", None),
        P("fsdp"),
        P(("dp", "fsdp"), "seq", None),
    )
    return jax.shard_map(
        local,
        mesh=mesh,
        in_specs=placed,
        out_specs=(
            P(("dp", "fsdp"), "seq", None),
            P(("dp", "fsdp"), "seq", None),
            P("fsdp", None),
            P("fsdp"),
            P("fsdp", None),
            P("fsdp", None),
            P("fsdp"),
            P("fsdp", None),
            P("fsdp"),
            P("fsdp"),
            P("fsdp"),
            P("fsdp", None),
            P("fsdp"),
            P("fsdp", None),
            P("fsdp"),
            P("fsdp"),
            P("fsdp"),
            P("fsdp", None),
            P("fsdp"),
        ),
        check_vma=False,
    )
```
